32 devices in a mesh: clips: 2 (over y), frame: 4 (over z), head: 2 (over x), seq: 2 (over core).
Axes of the slice: x: 2, y: 2, z: 4, core: 2. Of those that a mesh axis runs over, the one named last changes fastest.
Arguments:
- queries: bfloat16 [32, 1024, 1536], P(('clips', 'frame'), 'seq', 'head'), parts along dimension 0, may hold values from -150 to 150, as said below
- key_rows: bfloat16 [32, 1024, 1536], P(('clips', 'frame'), 'seq', 'head'), parts along dimension 0, may hold values from -5 to 5, as said below
- value_rows: bfloat16 [32, 1024, 1536], P(('clips', 'frame'), 'seq', 'head'), parts along dimension 0, may hold values from -6 to 6
- list_one: int32 [32, 2, 4], P('clips'), parts along dimension 0, may hold values from 0 to 7, as said below
- list_two: int32 [32, 2, 2], P('clips'), parts along dimension 0, may hold values from 0 to 7, as said below
- list_four: int32 [32, 2, 1], P('clips'), parts along dimension 0, may hold values from 0 to 7, as said below
- tile_counts: int32 [32, 2, 3], P('clips'), parts along dimension 0, may hold values from 0 to 4, as said below
Outputs:
- attended: bfloat16 [32, 1024, 1536], P(('clips', 'frame'), 'seq', 'head'), parts along dimension 0
The draws below stay inside these ranges and needn't reach their ends.
There are 2 independent parts, one for each index of `clips`. The reference program is written for one: setup_inputs(seed, part) draws one part's arguments, and reference() takes and returns one part's arrays. A program takes and returns all parts, laid end to end along the dimension named above; each array names one. Nothing has to cross between parts.
Inputs may be any that keep to these rules, and one draw needn't show every extreme that they name: Real-valued queries; a few query rows of a frame may be far larger in magnitude than the others. `key_rows`: Real-valued keys of order one. The entries of list_one[f, e, :] are distinct tile numbers of the frame f - 1 (e = 0) or f + 1 (e = 1). The entries of list_two[f, e, :] are distinct tile numbers of the frame f - 2 (e = 0) or f + 2 (e = 1). The entries of list_four[f, e, :] are distinct tile numbers of the frame f - 4 (e = 0) or f + 4 (e = 1). tile_counts[f, e, j] counts the live leading entries of the list of distance 1, 2, 4 (j = 0, 1, 2) for frame f and direction e; it is 0 exactly where the source frame lies outside the clip, else at least 1 and at most that list's length; frame 0's lists toward later frames are full.
All inputs are finite; a program needn't handle non-finite values.
Results may differ from the reference program's by a relative error of at most 0.0032.
Values may be sent and summed in bfloat16 or wider, within the bound.
A program may use at most 128 MiB of HBM per device.

```python
import jax
import jax.numpy as jnp
from jax import lax

HEADS = 12
HEAD_DIM = 128
FRAME_TILES = 8
TILE_TOKENS = 128
FRAMES = 16
FRAME_TOKENS = 1024
LIST_ONE = 4
LIST_TWO = 2
LIST_FOUR = 1


def paired_fields(key):
    shape = (FRAMES, FRAME_TOKENS, HEADS * HEAD_DIM)
    key_field = jnp.clip(jax.random.normal(jax.random.fold_in(key, 12), shape, jnp.float32), -5.0, 5.0)
    query_field = jnp.clip(2.5 * jax.random.normal(jax.random.fold_in(key, 11), shape, jnp.float32), -15.0, 15.0)
    return (query_field, key_field)


def draw_queries(key, part):
    return paired_fields(key)[0].astype(jnp.bfloat16)


def draw_key_rows(key, part):
    return paired_fields(key)[1].astype(jnp.bfloat16)


def tile_choice(key, length):
    ranking = jax.random.randint(key, (FRAMES, 2, FRAME_TILES), 0, 2 ** 20) * FRAME_TILES
    ranking = ranking + jnp.arange(FRAME_TILES, dtype=jnp.int32)[None, None, :]
    ordering = jnp.argsort(ranking, axis=2, stable=True)
    return ordering[:, :, :length].astype(jnp.int32)


def draw_list_one(key, part):
    return tile_choice(jax.random.fold_in(key, 21), LIST_ONE)


def draw_list_two(key, part):
    return tile_choice(jax.random.fold_in(key, 22), LIST_TWO)


def draw_list_four(key, part):
    return tile_choice(jax.random.fold_in(key, 23), LIST_FOUR)


def draw_tile_counts(key, part):
    upper = jnp.array([LIST_ONE, LIST_TWO, LIST_FOUR], jnp.int32)
    counted = jax.random.randint(jax.random.fold_in(key, 31), (FRAMES, 2, 3), 1, upper[None, None, :] + 1)
    frame_index = jnp.arange(FRAMES, dtype=jnp.int32)[:, None, None]
    distances = jnp.array([1, 2, 4], jnp.int32)[None, None, :]
    signs = (jnp.arange(2, dtype=jnp.int32) * 2 - 1)[None, :, None]
    target = frame_index + signs * distances
    inside_clip = (target >= 0) & (target < FRAMES)
    counted = jnp.where(inside_clip, counted, 0)
    counted = counted.at[0, 1, :].set(upper)
    return counted.astype(jnp.int32)


def levels(stream_key, dims, pieces, least, largest):
    level = 1.0
    for position, blocks in pieces:
        steps = jax.random.uniform(jax.random.fold_in(jax.random.fold_in(stream_key, 6), position), (blocks,), jnp.float32, least / len(pieces), largest / len(pieces))
        level = level * jnp.repeat(jnp.exp(steps), dims[position] // blocks).reshape((-1,) + (1,) * (len(dims) - 1 - position))
    return level


def noise(stream_key, dims, spread, most, shards=(), held_as=jnp.bfloat16):
    factor_of = levels(stream_key, dims, shards, -0.22, 0.18) if shards else 1.0
    result = jax.random.normal(stream_key, dims, jnp.float32) * spread * factor_of
    return jnp.minimum(jnp.maximum(result, -most), most).astype(held_as)


def setup_inputs(seed: int = 0, part: int = 0) -> dict:
    streams_of = jax.random.split(jax.random.key(seed), 8)
    part_splits = jax.random.split(jax.random.fold_in(streams_of[7], part), 8)
    return {
        "queries": draw_queries(jax.random.fold_in(jax.random.fold_in(streams_of[7], part), 71), part),
        "key_rows": draw_key_rows(jax.random.fold_in(jax.random.fold_in(streams_of[7], part), 71), part),
        "value_rows": noise(part_splits[2], (FRAMES, FRAME_TOKENS, HEADS * HEAD_DIM), 1.0, 6.0, ((0, 4), (1, 2), (2, 2))),
        "list_one": draw_list_one(jax.random.fold_in(jax.random.fold_in(streams_of[7], part), 71), part),
        "list_two": draw_list_two(jax.random.fold_in(jax.random.fold_in(streams_of[7], part), 71), part),
        "list_four": draw_list_four(jax.random.fold_in(jax.random.fold_in(streams_of[7], part), 71), part),
        "tile_counts": draw_tile_counts(jax.random.fold_in(jax.random.fold_in(streams_of[7], part), 71), part),
    }


def attend_one(frame, queries, key_rows, value_rows, list_one, list_two, list_four, tile_counts):
    width = key_rows.shape[2]
    key_tiles = key_rows.reshape(FRAMES, FRAME_TILES, TILE_TOKENS, width)
    value_tiles = value_rows.reshape(FRAMES, FRAME_TILES, TILE_TOKENS, width)
    key_parts = [key_rows[frame]]
    value_parts = [value_rows[frame]]
    live_parts = [jnp.ones((FRAME_TOKENS,), jnp.int32)]
    reaches = ((1, list_one), (2, list_two), (4, list_four))
    for direction in (0, 1):
        for slot_index, (distance, tile_list) in enumerate(reaches):
            source = jnp.clip(frame + (2 * direction - 1) * distance, 0, FRAMES - 1).astype(jnp.int32)
            chosen = tile_list[frame, direction]
            length = chosen.shape[0]
            key_parts.append(key_tiles[source][chosen].reshape(length * TILE_TOKENS, width))
            value_parts.append(value_tiles[source][chosen].reshape(length * TILE_TOKENS, width))
            slot_rank = jnp.arange(length * TILE_TOKENS, dtype=jnp.int32) // TILE_TOKENS
            live_parts.append((slot_rank < tile_counts[frame, direction, slot_index]).astype(jnp.int32))
    key_set = jnp.concatenate(key_parts, axis=0).astype(jnp.float32).reshape(-1, HEADS, HEAD_DIM)
    value_set = jnp.concatenate(value_parts, axis=0).astype(jnp.float32).reshape(-1, HEADS, HEAD_DIM)
    live_slots = jnp.concatenate(live_parts, axis=0)
    query_set = queries[frame].astype(jnp.float32).reshape(FRAME_TOKENS, HEADS, HEAD_DIM)
    score_scale = HEAD_DIM ** -0.5
    scores = jnp.einsum("thd,shd->hts", query_set, key_set, precision=lax.Precision.HIGHEST) * score_scale
    scores = jnp.where(live_slots[None, None, :] > 0, scores, -jnp.inf)
    row_max = jnp.max(scores, axis=2, keepdims=True)
    exponent = jnp.exp(scores - row_max)
    row_total = jnp.sum(exponent, axis=2, keepdims=True)
    rounded = lax.optimization_barrier(exponent.astype(jnp.bfloat16)).astype(jnp.float32)
    mixed_heads = jnp.einsum("hts,shd->htd", rounded, value_set, precision=lax.Precision.HIGHEST) / row_total
    return jnp.transpose(mixed_heads, (1, 0, 2)).reshape(FRAME_TOKENS, width).astype(jnp.bfloat16)


def reference(queries, key_rows, value_rows, list_one, list_two, list_four, tile_counts):
    def per_frame(frame):
        return attend_one(frame, queries, key_rows, value_rows, list_one, list_two, list_four, tile_counts)

    return lax.map(per_frame, jnp.arange(FRAMES, dtype=jnp.int32))
```

```python
import functools

import jax
import jax.numpy as jnp
from jax import lax
from jax.experimental import pallas as pl
from jax.experimental.pallas import tpu as pltpu
from jax.sharding import PartitionSpec as P

HEAD_DIM = 128
TILE = 128
DISTANCES = (1, 2, 4)
SCORE_SCALE = HEAD_DIM ** (-0.5) * 1.4426950408889634
GROUP = 4
ANY = pl.BlockSpec(memory_space=pl.ANY)


def list_at(lists, lengths, rank, frame, direction, entry):
    return lists[rank][(frame * 2 + direction) * lengths[rank] + entry]


def boundary_slots(lengths):
    return [
        (rank, distance, j, entry)
        for rank, distance in enumerate(DISTANCES)
        for j in range(distance)
        for entry in range(lengths[rank])
    ]


def pack_kernel(frames, frame_total, lengths, l1, l2, l4, k_own, k_other, v_own, v_other, up, down, sems):
    seq = lax.axis_index("seq")
    first = lax.axis_index("frame") * frames
    lists = (l1, l2, l4)
    half_tiles = k_own.shape[1] // TILE
    slots = boundary_slots(lengths)
    for direction, out in ((0, up), (1, down)):
        for slot, (rank, distance, j, entry) in enumerate(slots):
            if direction == 0:
                source, target = frames - distance + j, first + frames + j
            else:
                source, target = j, first - distance + j
            target = jnp.clip(target, 0, frame_total - 1)
            tile = list_at(lists, lengths, rank, target, direction, entry)
            mine = (tile // half_tiles) == seq
            rows = pl.ds(pl.multiple_of((tile % half_tiles) * TILE, TILE), TILE)
            sem = sems.at[direction * len(slots) + slot]
            for core, own, other in ((0, k_own, k_other), (1, v_own, v_other)):
                for local, ref in ((True, own), (False, other)):
                    wanted = mine if local else jnp.logical_not(mine)

                    @pl.when((seq == core) & wanted)
                    def _(ref=ref, source=source, rows=rows, out=out, slot=slot, sem=sem):
                        pltpu.make_async_copy(ref.at[source, rows, :], out.at[slot], sem).start()

    for direction, out in ((0, up), (1, down)):
        for slot in range(len(slots)):
            pltpu.make_async_copy(
                k_own.at[0, pl.ds(0, TILE), :], out.at[slot], sems.at[direction * len(slots) + slot]
            ).wait()


def scores_of(query, keys):
    return lax.dot_general(query, keys, (((1,), (1,)), ((), ())), preferred_element_type=jnp.float32)


def widened(values):
    return jnp.concatenate([values, jnp.ones_like(values)], axis=1)


def row_max(scores):
    return jnp.broadcast_to(jnp.max(scores, axis=1, keepdims=True), (scores.shape[0], HEAD_DIM))


def weights_of(scores, top):
    repeats = scores.shape[1] // HEAD_DIM
    return jnp.exp2((scores - jnp.concatenate([top] * repeats, axis=1)) * SCORE_SCALE).astype(jnp.bfloat16)


def columns(head):
    return slice(head * HEAD_DIM, (head + 1) * HEAD_DIM)


def listed_chunks(chosen, count, heads, base, q_ref, kbuf, vbuf, acc, top):
    def chunk(step, carry):
        ids = [chosen[step * GROUP + place] for place in range(GROUP)]
        spans = [pl.ds(pl.multiple_of(i * TILE, TILE), TILE) for i in ids]
        biases = [
            jnp.where(step * GROUP + place < count, jnp.float32(0.0), jnp.float32(-jnp.inf))
            for place in range(GROUP)
        ]
        all_scores = []
        for head in range(heads):
            cols = pl.ds(pl.multiple_of(base + head * HEAD_DIM, HEAD_DIM), HEAD_DIM)
            keys = jnp.concatenate([kbuf[span, cols] for span in spans], axis=0)
            scores = scores_of(q_ref[0, :, columns(head)], keys)
            parts = [scores[:, :TILE]] + [
                scores[:, place * TILE : (place + 1) * TILE] + biases[place] for place in range(1, GROUP)
            ]
            all_scores.append(jnp.concatenate(parts, axis=1))
        for head in range(heads):
            cols = pl.ds(pl.multiple_of(base + head * HEAD_DIM, HEAD_DIM), HEAD_DIM)
            values = jnp.concatenate([vbuf[span, cols] for span in spans], axis=0)
            old = top[head]
            new = jnp.maximum(old, row_max(all_scores[head]))
            factor = jnp.exp2((old - new) * SCORE_SCALE)
            weights = weights_of(all_scores[head], new)
            mixed = jnp.dot(weights, widened(values), preferred_element_type=jnp.float32)
            acc[head] = acc[head] * jnp.concatenate([factor, factor], axis=1) + mixed
            top[head] = new
        return carry

    lax.fori_loop(0, (count + GROUP - 1) // GROUP, chunk, 0)


def near_kernel(
    frames, heads, lengths, l1, l2, l4, counts, q_ref, k_own, k_other, v_own, v_other,
    acc_out, state_out, kbuf, vbuf, acc, top, chosen, sems,
):
    seq = lax.axis_index("seq")
    frame, group = pl.program_id(0), pl.program_id(1)
    half = k_own.shape[1]
    frame_tokens = 2 * half
    lists = (l1, l2, l4)

    def copies(source):
        for place, (ref, buf, owner) in enumerate(
            ((k_own, kbuf, seq), (k_other, kbuf, 1 - seq), (v_own, vbuf, seq), (v_other, vbuf, 1 - seq))
        ):
            rows = pl.ds(pl.multiple_of(source * frame_tokens + owner * half, half), half)
            yield pltpu.make_async_copy(ref.at[source], buf.at[rows, :], sems.at[source, place])

    @pl.when((frame == 0) & (group == 0))
    def _():
        for source in range(frames):
            for copy in copies(source):
                copy.start()
        for source in range(frames):
            for copy in copies(source):
                copy.wait()

    count = jnp.int32(0)
    mine = lax.axis_index("frame") * frames + frame
    for direction in (0, 1):
        for rank, distance in enumerate(DISTANCES):
            if distance >= frames:
                continue
            source = frame + (2 * direction - 1) * distance
            inside = (source >= 0) & (source < frames)
            live = counts[(mine * 2 + direction) * len(DISTANCES) + rank]
            for entry in range(lengths[rank]):
                tile = list_at(lists, lengths, rank, mine, direction, entry)
                keep = inside & (entry < live)
                chosen[count] = jnp.where(keep, source * (frame_tokens // TILE) + tile, 0)
                count = count + keep.astype(jnp.int32)
    for place in range(GROUP):
        chosen[count + place] = 0

    base = group * heads * HEAD_DIM
    rows = pl.ds(pl.multiple_of(frame * frame_tokens, frame_tokens), frame_tokens)

    def cols_of(head):
        return pl.ds(pl.multiple_of(base + head * HEAD_DIM, HEAD_DIM), HEAD_DIM)

    scores = scores_of(q_ref[0, :, columns(0)], kbuf[rows, cols_of(0)])
    for head in range(heads):
        following = None
        if head + 1 < heads:
            following = scores_of(q_ref[0, :, columns(head + 1)], kbuf[rows, cols_of(head + 1)])
        new = row_max(scores)
        acc[head] = jnp.dot(
            weights_of(scores, new), widened(vbuf[rows, cols_of(head)]), preferred_element_type=jnp.float32
        )
        top[head] = new
        scores = following
    listed_chunks(chosen, count, heads, base, q_ref, kbuf, vbuf, acc, top)
    lane = lax.broadcasted_iota(jnp.int32, (half, HEAD_DIM), 1)
    state = jnp.zeros((half, HEAD_DIM), jnp.float32)
    for head in range(heads):
        acc_out[0, :, columns(head)] = acc[head, :, :HEAD_DIM]
        state = jnp.where(lane == 2 * head, top[head], state)
        state = jnp.where(lane == 2 * head + 1, acc[head, :, HEAD_DIM:], state)
    state_out[0, 0] = state


def far_kernel(
    frames, heads, lengths, counts, q_ref, acc_in, state_in, up_own, up_other, down_own, down_other,
    out_ref, kbuf, vbuf, acc, top, chosen, sems,
):
    seq = lax.axis_index("seq")
    frame, group = pl.program_id(0), pl.program_id(1)
    rows = up_own.shape[0]
    half = q_ref.shape[1]
    slots = boundary_slots(lengths)

    def copies(core):
        for place, (own, other) in enumerate(((up_own, up_other), (down_own, down_other))):
            keys, values = (own, other) if core == 0 else (other, own)
            span = pl.ds(place * rows, rows)
            yield pltpu.make_async_copy(keys, kbuf.at[span, :], sems.at[2 * place])
            yield pltpu.make_async_copy(values, vbuf.at[span, :], sems.at[2 * place + 1])

    for core in (0, 1):

        @pl.when((frame == 0) & (group == 0) & (seq == core))
        def _(core=core):
            for copy in copies(core):
                copy.start()
            for copy in copies(core):
                copy.wait()

    count = jnp.int32(0)
    mine = lax.axis_index("frame") * frames + frame
    for direction in (0, 1):
        start = direction * len(slots)
        for rank, distance in enumerate(DISTANCES):
            place = frame if direction == 0 else frame - (frames - distance)
            crosses = (place >= 0) & (place < distance)
            live = counts[(mine * 2 + direction) * len(DISTANCES) + rank]
            for entry in range(lengths[rank]):
                keep = crosses & (entry < live)
                chosen[count] = jnp.where(keep, start + place * lengths[rank] + entry, 0)
                count = count + keep.astype(jnp.int32)
            start += distance * lengths[rank]
    for place in range(GROUP):
        chosen[count + place] = 0

    state = state_in[0, 0]
    for head in range(heads):
        acc[head, :, :HEAD_DIM] = acc_in[0, :, columns(head)]
        acc[head, :, HEAD_DIM:] = jnp.broadcast_to(state[:, 2 * head + 1 : 2 * head + 2], (half, HEAD_DIM))
        top[head] = jnp.broadcast_to(state[:, 2 * head : 2 * head + 1], (half, HEAD_DIM))
    listed_chunks(chosen, count, heads, group * heads * HEAD_DIM, q_ref, kbuf, vbuf, acc, top)
    for head in range(heads):
        out_ref[0, :, columns(head)] = (acc[head, :, :HEAD_DIM] / acc[head, :, HEAD_DIM:]).astype(jnp.bfloat16)


def per_device(queries, key_rows, value_rows, list_one, list_two, list_four, tile_counts):
    frames, half, width = queries.shape
    frame_total = list_one.shape[0]
    lengths = (list_one.shape[2], list_two.shape[2], list_four.shape[2])
    head_total = width // HEAD_DIM
    heads = max(h for h in (1, 2, 3) if head_total % h == 0)
    groups = head_total // heads
    slots = len(boundary_slots(lengths))
    lists = tuple(x.reshape(-1) for x in (list_one, list_two, list_four))
    counts = tile_counts.reshape(-1)
    listed = 2 * sum(lengths)
    devices = lax.axis_size("frame")
    swap = [(0, 1), (1, 0)]

    k_other = lax.ppermute(key_rows, "seq", swap)
    v_other = lax.ppermute(value_rows, "seq", swap)

    packed = jax.ShapeDtypeStruct((slots, TILE, width), jnp.bfloat16)
    whole = pl.BlockSpec(memory_space=pltpu.VMEM)
    up, down = pl.pallas_call(
        functools.partial(pack_kernel, frames, frame_total, lengths),
        out_shape=(packed, packed),
        in_specs=[pl.BlockSpec(memory_space=pltpu.SMEM)] * 3 + [ANY] * 4,
        out_specs=(whole, whole),
        scratch_shapes=[pltpu.SemaphoreType.DMA((2 * slots,))],
        name="pack",
    )(*lists, key_rows, k_other, value_rows, v_other)

    up = lax.ppermute(up, "frame", [(i, i + 1) for i in range(devices - 1)])
    down = lax.ppermute(down, "frame", [(i + 1, i) for i in range(devices - 1)])
    up = up.reshape(slots * TILE, width)
    down = down.reshape(slots * TILE, width)
    up_other = lax.ppermute(up, "seq", swap)
    down_other = lax.ppermute(down, "seq", swap)

    def cost(tokens):
        return pl.CostEstimate(
            flops=8 * frames * half * width * tokens,
            transcendentals=frames * half * head_total * tokens,
            bytes_accessed=40 * frames * half * width,
        )

    def block(f, g, *_):
        return (f, 0, g)

    q_spec = pl.BlockSpec((1, half, heads * HEAD_DIM), block)
    state_spec = pl.BlockSpec((1, 1, half, HEAD_DIM), lambda f, g, *_: (f, g, 0, 0))
    running = [
        pltpu.VMEM((heads, half, 2 * HEAD_DIM), jnp.float32),
        pltpu.VMEM((heads, half, HEAD_DIM), jnp.float32),
        pltpu.SMEM((listed + GROUP,), jnp.int32),
    ]
    params = pltpu.CompilerParams(vmem_limit_bytes=60 << 20)
    acc, state = pl.pallas_call(
        functools.partial(near_kernel, frames, heads, lengths),
        grid_spec=pltpu.PrefetchScalarGridSpec(
            num_scalar_prefetch=4,
            grid=(frames, groups),
            in_specs=[q_spec] + [ANY] * 4,
            out_specs=(q_spec, state_spec),
            scratch_shapes=[pltpu.VMEM((frames * 2 * half, width), jnp.bfloat16)] * 2
            + running
            + [pltpu.SemaphoreType.DMA((frames, 4))],
        ),
        out_shape=(
            jax.ShapeDtypeStruct(queries.shape, jnp.float32),
            jax.ShapeDtypeStruct((frames, groups, half, HEAD_DIM), jnp.float32),
        ),
        compiler_params=params,
        cost_estimate=cost(2 * half + listed * TILE // 2),
        name="near",
    )(*lists, counts, queries, key_rows, k_other, value_rows, v_other)

    return pl.pallas_call(
        functools.partial(far_kernel, frames, heads, lengths),
        grid_spec=pltpu.PrefetchScalarGridSpec(
            num_scalar_prefetch=1,
            grid=(frames, groups),
            in_specs=[q_spec, q_spec, state_spec] + [ANY] * 4,
            out_specs=q_spec,
            scratch_shapes=[pltpu.VMEM((2 * slots * TILE, width), jnp.bfloat16)] * 2
            + running
            + [pltpu.SemaphoreType.DMA((4,))],
        ),
        out_shape=jax.ShapeDtypeStruct(queries.shape, jnp.bfloat16),
        compiler_params=params,
        cost_estimate=cost(listed * TILE // 2),
        name="far",
    )(counts, queries, acc, state, up, up_other, down, down_other)


def solution(mesh):
    placed = P(("clips", "frame"), "seq", "head")
    listing = P("clips", None, None)
    return jax.shard_map(
        per_device,
        mesh=mesh,
        in_specs=(placed, placed, placed, listing, listing, listing, listing),
        out_specs=placed,
        check_vma=False,
    )
```

```python
import functools

import jax
import jax.numpy as jnp
from jax import lax
from jax.experimental import pallas as pl
from jax.experimental.pallas import tpu as pltpu
from jax.sharding import PartitionSpec as P

HEAD_DIM = 128
TILE = 128
DISTANCES = (1, 2, 4)
SCORE_SCALE = HEAD_DIM ** (-0.5) * 1.4426950408889634
GROUP = 4
ANY = pl.BlockSpec(memory_space=pl.ANY)


def list_at(lists, lengths, rank, frame, direction, entry):
    return lists[rank][(frame * 2 + direction) * lengths[rank] + entry]


def boundary_slots(lengths, direction, edge):
    return [
        (rank, distance, j, entry)
        for rank, distance in enumerate(DISTANCES)
        for j in range(distance)
        if edge == (j == (0 if direction == 0 else distance - 1))
        for entry in range(lengths[rank])
    ]


def parts_of(lengths):
    return [(direction, boundary_slots(lengths, direction, edge)) for edge in (False, True) for direction in (0, 1)]


def pack_kernel(frames, frame_total, lengths, l1, l2, l4, k_own, k_other, v_own, v_other, *outs_and_sems):
    seq = lax.axis_index("seq")
    first = lax.axis_index("frame") * frames
    lists = (l1, l2, l4)
    half_tiles = k_own.shape[1] // TILE
    *outs, sems = outs_and_sems
    waits = []
    for (direction, slots), out in zip(parts_of(lengths), outs):
        for slot, (rank, distance, j, entry) in enumerate(slots):
            if direction == 0:
                source, target = frames - distance + j, first + frames + j
            else:
                source, target = j, first - distance + j
            target = jnp.clip(target, 0, frame_total - 1)
            tile = list_at(lists, lengths, rank, target, direction, entry)
            mine = (tile // half_tiles) == seq
            rows = pl.ds(pl.multiple_of((tile % half_tiles) * TILE, TILE), TILE)
            sem = sems.at[len(waits)]
            waits.append(pltpu.make_async_copy(k_own.at[0, pl.ds(0, TILE), :], out.at[slot], sem))
            for core, own, other in ((0, k_own, k_other), (1, v_own, v_other)):
                for local, ref in ((True, own), (False, other)):
                    wanted = mine if local else jnp.logical_not(mine)

                    @pl.when((seq == core) & wanted)
                    def _(ref=ref, source=source, rows=rows, out=out, slot=slot, sem=sem):
                        pltpu.make_async_copy(ref.at[source, rows, :], out.at[slot], sem).start()

    for wait in waits:
        wait.wait()


def scores_of(query, keys):
    return lax.dot_general(query, keys, (((1,), (1,)), ((), ())), preferred_element_type=jnp.float32)


def widened(values):
    return jnp.concatenate([values, jnp.ones_like(values)], axis=1)


def row_max(scores):
    return jnp.broadcast_to(jnp.max(scores, axis=1, keepdims=True), (scores.shape[0], HEAD_DIM))


def weights_of(scores, top):
    repeats = scores.shape[1] // HEAD_DIM
    return jnp.exp2((scores - jnp.concatenate([top] * repeats, axis=1)) * SCORE_SCALE).astype(jnp.bfloat16)


def columns(head):
    return slice(head * HEAD_DIM, (head + 1) * HEAD_DIM)


def listed_chunks(chosen, count, heads, base, q_ref, kbuf, vbuf, acc, top):
    def chunk(step, carry):
        ids = [chosen[step * GROUP + place] for place in range(GROUP)]
        spans = [pl.ds(pl.multiple_of(i * TILE, TILE), TILE) for i in ids]
        biases = [
            jnp.where(step * GROUP + place < count, jnp.float32(0.0), jnp.float32(-jnp.inf))
            for place in range(GROUP)
        ]
        all_scores = []
        for head in range(heads):
            cols = pl.ds(pl.multiple_of(base + head * HEAD_DIM, HEAD_DIM), HEAD_DIM)
            keys = jnp.concatenate([kbuf[span, cols] for span in spans], axis=0)
            scores = scores_of(q_ref[0, :, columns(head)], keys)
            parts = [scores[:, :TILE]] + [
                scores[:, place * TILE : (place + 1) * TILE] + biases[place] for place in range(1, GROUP)
            ]
            all_scores.append(jnp.concatenate(parts, axis=1))
        for head in range(heads):
            cols = pl.ds(pl.multiple_of(base + head * HEAD_DIM, HEAD_DIM), HEAD_DIM)
            values = jnp.concatenate([vbuf[span, cols] for span in spans], axis=0)
            old = top[head]
            new = jnp.maximum(old, row_max(all_scores[head]))
            factor = jnp.exp2((old - new) * SCORE_SCALE)
            weights = weights_of(all_scores[head], new)
            mixed = jnp.dot(weights, widened(values), preferred_element_type=jnp.float32)
            acc[head] = acc[head] * jnp.concatenate([factor, factor], axis=1) + mixed
            top[head] = new
        return carry

    lax.fori_loop(0, (count + GROUP - 1) // GROUP, chunk, 0)


def near_kernel(
    frames, heads, lengths, l1, l2, l4, counts, q_ref, k_own, k_other, v_own, v_other,
    acc_out, state_out, kbuf, vbuf, acc, top, chosen, sems,
):
    seq = lax.axis_index("seq")
    frame, group = pl.program_id(0), pl.program_id(1)
    half = k_own.shape[1]
    frame_tokens = 2 * half
    lists = (l1, l2, l4)

    def copies(source):
        for place, (ref, buf, owner) in enumerate(
            ((k_own, kbuf, seq), (k_other, kbuf, 1 - seq), (v_own, vbuf, seq), (v_other, vbuf, 1 - seq))
        ):
            rows = pl.ds(pl.multiple_of(source * frame_tokens + owner * half, half), half)
            yield pltpu.make_async_copy(ref.at[source], buf.at[rows, :], sems.at[source, place])

    @pl.when((frame == 0) & (group == 0))
    def _():
        for source in range(frames):
            for copy in copies(source):
                copy.start()

    reach = max([0] + [distance for distance in DISTANCES if distance < frames])

    def arrived(at_frame, sources):
        @pl.when((frame == at_frame) & (group == 0))
        def _():
            for source in sources:
                for copy in copies(source):
                    copy.wait()

    arrived(0, range(1))
    count = jnp.int32(0)
    mine = lax.axis_index("frame") * frames + frame
    for direction in (0, 1):
        for rank, distance in enumerate(DISTANCES):
            if distance >= frames:
                continue
            source = frame + (2 * direction - 1) * distance
            inside = (source >= 0) & (source < frames)
            live = counts[(mine * 2 + direction) * len(DISTANCES) + rank]
            for entry in range(lengths[rank]):
                tile = list_at(lists, lengths, rank, mine, direction, entry)
                keep = inside & (entry < live)
                chosen[count] = jnp.where(keep, source * (frame_tokens // TILE) + tile, 0)
                count = count + keep.astype(jnp.int32)
    for place in range(GROUP):
        chosen[count + place] = 0

    base = group * heads * HEAD_DIM
    rows = pl.ds(pl.multiple_of(frame * frame_tokens, frame_tokens), frame_tokens)

    def cols_of(head):
        return pl.ds(pl.multiple_of(base + head * HEAD_DIM, HEAD_DIM), HEAD_DIM)

    scores = scores_of(q_ref[0, :, columns(0)], kbuf[rows, cols_of(0)])
    for head in range(heads):
        following = None
        if head + 1 < heads:
            following = scores_of(q_ref[0, :, columns(head + 1)], kbuf[rows, cols_of(head + 1)])
        new = row_max(scores)
        acc[head] = jnp.dot(
            weights_of(scores, new), widened(vbuf[rows, cols_of(head)]), preferred_element_type=jnp.float32
        )
        top[head] = new
        scores = following
    arrived(0, range(1, min(reach, frames - 1) + 1))
    for at_frame in range(1, frames - reach):
        arrived(at_frame, [at_frame + reach])
    listed_chunks(chosen, count, heads, base, q_ref, kbuf, vbuf, acc, top)
    lane = lax.broadcasted_iota(jnp.int32, (half, HEAD_DIM), 1)
    state = jnp.zeros((half, HEAD_DIM), jnp.float32)
    for head in range(heads):
        acc_out[0, :, columns(head)] = acc[head, :, :HEAD_DIM]
        state = jnp.where(lane == 2 * head, top[head], state)
        state = jnp.where(lane == 2 * head + 1, acc[head, :, HEAD_DIM:], state)
    state_out[0, 0] = state


def far_kernel(frames, heads, lengths, edge, counts, q_ref, acc_in, state_in, *refs):
    parts = 4 if edge else 2
    owns, others, rest = refs[:parts], refs[parts : 2 * parts], refs[2 * parts + edge :]
    out_ref, kbuf, vbuf, acc, top, chosen, sems = rest
    seq = lax.axis_index("seq")
    step, group = pl.program_id(0), pl.program_id(1)
    frame = step * (frames - 1) if edge else step + 1
    half = q_ref.shape[1]
    behind = sum((distance - 1) * length for distance, length in zip(DISTANCES, lengths))
    beside = sum(lengths)

    def copies(core):
        first = 0
        for place, (own, other) in enumerate(zip(owns, others)):
            keys, values = (own, other) if core == 0 else (other, own)
            span = pl.ds(first, own.shape[0])
            first += own.shape[0]
            yield pltpu.make_async_copy(keys, kbuf.at[span, :], sems.at[2 * place])
            yield pltpu.make_async_copy(values, vbuf.at[span, :], sems.at[2 * place + 1])

    for core in (0, 1):

        @pl.when((step == 0) & (group == 0) & (seq == core))
        def _(core=core):
            for copy in copies(core):
                copy.start()

    count = jnp.int32(0)
    mine = lax.axis_index("frame") * frames + frame
    for direction in (0, 1):
        first_behind, first_beside = direction * behind, 2 * behind + direction * beside
        for rank, distance in enumerate(DISTANCES):
            place = frame if direction == 0 else frame - (frames - distance)
            next_to = frame == (0 if direction == 0 else frames - 1)
            crosses = (place >= 0) & (place < distance)
            live = counts[(mine * 2 + direction) * len(DISTANCES) + rank]
            for entry in range(lengths[rank]):
                keep = crosses & (entry < live)
                at = jnp.where(
                    next_to, first_beside + entry, first_behind + (place - (1 - direction)) * lengths[rank] + entry
                )
                chosen[count] = jnp.where(keep, at, 0)
                count = count + keep.astype(jnp.int32)
            first_behind += (distance - 1) * lengths[rank]
            first_beside += lengths[rank]
    for place in range(GROUP):
        chosen[count + place] = 0

    state = state_in[0, 0]
    for head in range(heads):
        acc[head, :, :HEAD_DIM] = acc_in[0, :, columns(head)]
        acc[head, :, HEAD_DIM:] = jnp.broadcast_to(state[:, 2 * head + 1 : 2 * head + 2], (half, HEAD_DIM))
        top[head] = jnp.broadcast_to(state[:, 2 * head : 2 * head + 1], (half, HEAD_DIM))
    for core in (0, 1):

        @pl.when((step == 0) & (group == 0) & (seq == core))
        def _(core=core):
            for copy in copies(core):
                copy.wait()

    listed_chunks(chosen, count, heads, group * heads * HEAD_DIM, q_ref, kbuf, vbuf, acc, top)
    for head in range(heads):
        out_ref[0, :, columns(head)] = (acc[head, :, :HEAD_DIM] / acc[head, :, HEAD_DIM:]).astype(jnp.bfloat16)


def per_device(queries, key_rows, value_rows, list_one, list_two, list_four, tile_counts):
    frames, half, width = queries.shape
    frame_total = list_one.shape[0]
    lengths = (list_one.shape[2], list_two.shape[2], list_four.shape[2])
    head_total = width // HEAD_DIM
    heads = max(h for h in (1, 2, 3) if head_total % h == 0)
    groups = head_total // heads
    parts = parts_of(lengths)
    slots = sum(len(part) for _, part in parts)
    lists = tuple(x.reshape(-1) for x in (list_one, list_two, list_four))
    counts = tile_counts.reshape(-1)
    listed = 2 * sum(lengths)
    devices = lax.axis_size("frame")
    swap = [(0, 1), (1, 0)]

    k_other = lax.ppermute(key_rows, "seq", swap)
    v_other = lax.ppermute(value_rows, "seq", swap)

    whole = pl.BlockSpec(memory_space=pltpu.VMEM)
    packed = pl.pallas_call(
        functools.partial(pack_kernel, frames, frame_total, lengths),
        out_shape=[jax.ShapeDtypeStruct((len(part), TILE, width), jnp.bfloat16) for _, part in parts],
        in_specs=[pl.BlockSpec(memory_space=pltpu.SMEM)] * 3 + [ANY] * 4,
        out_specs=[whole] * len(parts),
        scratch_shapes=[pltpu.SemaphoreType.DMA((slots,))],
        name="pack",
    )(*lists, key_rows, k_other, value_rows, v_other)

    routes = ([(i, i + 1) for i in range(devices - 1)], [(i + 1, i) for i in range(devices - 1)])
    sent = [
        lax.ppermute(x.reshape(-1, width), "frame", routes[direction]) for x, (direction, _) in zip(packed, parts)
    ]

    def cost(tokens):
        return pl.CostEstimate(
            flops=8 * frames * half * width * tokens,
            transcendentals=frames * half * head_total * tokens,
            bytes_accessed=40 * frames * half * width,
        )

    def block(f, g, *_):
        return (f, 0, g)

    q_spec = pl.BlockSpec((1, half, heads * HEAD_DIM), block)
    state_spec = pl.BlockSpec((1, 1, half, HEAD_DIM), lambda f, g, *_: (f, g, 0, 0))
    running = [
        pltpu.VMEM((heads, half, 2 * HEAD_DIM), jnp.float32),
        pltpu.VMEM((heads, half, HEAD_DIM), jnp.float32),
        pltpu.SMEM((listed + GROUP,), jnp.int32),
    ]
    params = pltpu.CompilerParams(vmem_limit_bytes=60 << 20)
    acc, state = pl.pallas_call(
        functools.partial(near_kernel, frames, heads, lengths),
        grid_spec=pltpu.PrefetchScalarGridSpec(
            num_scalar_prefetch=4,
            grid=(frames, groups),
            in_specs=[q_spec] + [ANY] * 4,
            out_specs=(q_spec, state_spec),
            scratch_shapes=[pltpu.VMEM((frames * 2 * half, width), jnp.bfloat16)] * 2
            + running
            + [pltpu.SemaphoreType.DMA((frames, 4))],
        ),
        out_shape=(
            jax.ShapeDtypeStruct(queries.shape, jnp.float32),
            jax.ShapeDtypeStruct((frames, groups, half, HEAD_DIM), jnp.float32),
        ),
        compiler_params=params,
        cost_estimate=cost(2 * half + listed * TILE // 2),
        name="near",
    )(*lists, counts, queries, key_rows, k_other, value_rows, v_other)

    behind = lax.optimization_barrier((acc, *sent[:2]))
    beside = lax.optimization_barrier((acc, *sent[2:]))
    acc = behind[0]
    own = [*behind[1:], *beside[1:]]
    other = [lax.ppermute(x, "seq", swap) for x in own]

    def far(edge, frame_of, steps, done):
        used = 4 if edge else 2
        rows = sum(x.shape[0] for x in own[:used])
        far_block = lambda f, g, *_: (frame_of(f), 0, g)
        far_spec = pl.BlockSpec((1, half, heads * HEAD_DIM), far_block)
        far_state = pl.BlockSpec((1, 1, half, HEAD_DIM), lambda f, g, *_: (frame_of(f), g, 0, 0))
        return pl.pallas_call(
            functools.partial(far_kernel, frames, heads, lengths, edge),
            grid_spec=pltpu.PrefetchScalarGridSpec(
                num_scalar_prefetch=1,
                grid=(steps, groups),
                in_specs=[far_spec, far_spec, far_state] + [ANY] * (2 * used + len(done)),
                out_specs=far_spec,
                scratch_shapes=[pltpu.VMEM((rows, width), jnp.bfloat16)] * 2
                + running
                + [pltpu.SemaphoreType.DMA((2 * used,))],
            ),
            out_shape=jax.ShapeDtypeStruct(queries.shape, jnp.bfloat16),
            input_output_aliases={4 + 2 * used: 0} if done else {},
            compiler_params=params,
            cost_estimate=cost(listed * TILE // 4),
            name="far_edge" if edge else "far_inner",
        )(counts, queries, acc, state, *own[:used], *other[:used], *done)

    inner = far(False, lambda f: f + 1, frames - 2, ())
    return far(True, lambda f: f * (frames - 1), 2, (inner,))


def solution(mesh):
    placed = P(("clips", "frame"), "seq", "head")
    listing = P("clips", None, None)
    return jax.shard_map(
        per_device,
        mesh=mesh,
        in_specs=(placed, placed, placed, listing, listing, listing, listing),
        out_specs=placed,
        check_vma=False,
    )
```

```python
import functools

import jax
import jax.numpy as jnp
from jax import lax
from jax.experimental import pallas as pl
from jax.experimental.pallas import tpu as pltpu
from jax.sharding import PartitionSpec as P

HEAD_DIM = 128
TILE = 128
DISTANCES = (1, 2, 4)
SCORE_SCALE = HEAD_DIM ** (-0.5) * 1.4426950408889634
GROUP = 4
ANY = pl.BlockSpec(memory_space=pl.ANY)


def list_at(lists, lengths, rank, frame, direction, entry):
    return lists[rank][(frame * 2 + direction) * lengths[rank] + entry]


def boundary_slots(lengths, direction, edge):
    return [
        (rank, distance, j, entry)
        for rank, distance in enumerate(DISTANCES)
        for j in range(distance)
        if edge == (j == (0 if direction == 0 else distance - 1))
        for entry in range(lengths[rank])
    ]


def parts_of(lengths):
    return [(direction, boundary_slots(lengths, direction, edge)) for edge in (False, True) for direction in (0, 1)]


def pack_kernel(frames, frame_total, lengths, l1, l2, l4, k_own, k_other, v_own, v_other, *outs_and_sems):
    seq = lax.axis_index("seq")
    first = lax.axis_index("frame") * frames
    lists = (l1, l2, l4)
    half_tiles = k_own.shape[1] // TILE
    *outs, sems = outs_and_sems
    waits = []
    for (direction, slots), out in zip(parts_of(lengths), outs):
        for slot, (rank, distance, j, entry) in enumerate(slots):
            if direction == 0:
                source, target = frames - distance + j, first + frames + j
            else:
                source, target = j, first - distance + j
            target = jnp.clip(target, 0, frame_total - 1)
            tile = list_at(lists, lengths, rank, target, direction, entry)
            mine = (tile // half_tiles) == seq
            rows = pl.ds(pl.multiple_of((tile % half_tiles) * TILE, TILE), TILE)
            sem = sems.at[len(waits)]
            waits.append(pltpu.make_async_copy(k_own.at[0, pl.ds(0, TILE), :], out.at[slot], sem))
            for core, own, other in ((0, k_own, k_other), (1, v_own, v_other)):
                for local, ref in ((True, own), (False, other)):
                    wanted = mine if local else jnp.logical_not(mine)

                    @pl.when((seq == core) & wanted)
                    def _(ref=ref, source=source, rows=rows, out=out, slot=slot, sem=sem):
                        pltpu.make_async_copy(ref.at[source, rows, :], out.at[slot], sem).start()

    for wait in waits:
        wait.wait()


def scores_of(query, keys):
    return lax.dot_general(query, keys, (((1,), (1,)), ((), ())), preferred_element_type=jnp.float32)


def widened(values):
    return jnp.concatenate([values, jnp.ones_like(values)], axis=1)


def row_max(scores):
    return jnp.broadcast_to(jnp.max(scores, axis=1, keepdims=True), (scores.shape[0], HEAD_DIM))


def weights_of(scores, top):
    repeats = scores.shape[1] // HEAD_DIM
    return jnp.exp2((scores - jnp.concatenate([top] * repeats, axis=1)) * SCORE_SCALE).astype(jnp.bfloat16)


def columns(head):
    return slice(head * HEAD_DIM, (head + 1) * HEAD_DIM)


def listed_chunks(chosen, count, heads, base, q_ref, kbuf, vbuf, acc, top):
    def chunk(step, carry):
        ids = [chosen[step * GROUP + place] for place in range(GROUP)]
        spans = [pl.ds(pl.multiple_of(i * TILE, TILE), TILE) for i in ids]
        biases = [
            jnp.where(step * GROUP + place < count, jnp.float32(0.0), jnp.float32(-jnp.inf))
            for place in range(GROUP)
        ]
        all_scores = []
        for head in range(heads):
            cols = pl.ds(pl.multiple_of(base + head * HEAD_DIM, HEAD_DIM), HEAD_DIM)
            keys = jnp.concatenate([kbuf[span, cols] for span in spans], axis=0)
            scores = scores_of(q_ref[0, :, columns(head)], keys)
            parts = [scores[:, :TILE]] + [
                scores[:, place * TILE : (place + 1) * TILE] + biases[place] for place in range(1, GROUP)
            ]
            all_scores.append(jnp.concatenate(parts, axis=1))
        for head in range(heads):
            cols = pl.ds(pl.multiple_of(base + head * HEAD_DIM, HEAD_DIM), HEAD_DIM)
            values = jnp.concatenate([vbuf[span, cols] for span in spans], axis=0)
            old = top[head]
            new = jnp.maximum(old, row_max(all_scores[head]))
            factor = jnp.exp2((old - new) * SCORE_SCALE)
            weights = weights_of(all_scores[head], new)
            mixed = jnp.dot(weights, widened(values), preferred_element_type=jnp.float32)
            acc[head] = acc[head] * jnp.concatenate([factor, factor], axis=1) + mixed
            top[head] = new
        return carry

    lax.fori_loop(0, (count + GROUP - 1) // GROUP, chunk, 0)


def near_kernel(
    frames, heads, lengths, l1, l2, l4, counts, q_ref, k_own, v_own, k_first, v_first, k_second, v_second,
    acc_out, state_out, kbuf, vbuf, acc, top, chosen, sems,
):
    seq = lax.axis_index("seq")
    frame, group = pl.program_id(0), pl.program_id(1)
    half = k_own.shape[1]
    frame_tokens = 2 * half
    lists = (l1, l2, l4)

    def copies(source, core):
        k_other, v_other = (k_first, v_second) if core == 0 else (k_second, v_first)
        for place, (ref, buf, owner) in enumerate(
            ((k_own, kbuf, core), (k_other, kbuf, 1 - core), (v_own, vbuf, core), (v_other, vbuf, 1 - core))
        ):
            rows = pl.ds(pl.multiple_of(source * frame_tokens + owner * half, half), half)
            yield pltpu.make_async_copy(ref.at[source], buf.at[rows, :], sems.at[source, place])

    for core in (0, 1):

        @pl.when((frame == 0) & (group == 0) & (seq == core))
        def _(core=core):
            for source in range(frames):
                for copy in copies(source, core):
                    copy.start()

    reach = max([0] + [distance for distance in DISTANCES if distance < frames])

    def arrived(at_frame, sources):
        @pl.when((frame == at_frame) & (group == 0))
        def _():
            for source in sources:
                for copy in copies(source, 0):
                    copy.wait()

    arrived(0, range(1))
    count = jnp.int32(0)
    mine = lax.axis_index("frame") * frames + frame
    for direction in (0, 1):
        for rank, distance in enumerate(DISTANCES):
            if distance >= frames:
                continue
            source = frame + (2 * direction - 1) * distance
            inside = (source >= 0) & (source < frames)
            live = counts[(mine * 2 + direction) * len(DISTANCES) + rank]
            for entry in range(lengths[rank]):
                tile = list_at(lists, lengths, rank, mine, direction, entry)
                keep = inside & (entry < live)
                chosen[count] = jnp.where(keep, source * (frame_tokens // TILE) + tile, 0)
                count = count + keep.astype(jnp.int32)
    for place in range(GROUP):
        chosen[count + place] = 0

    base = group * heads * HEAD_DIM
    rows = pl.ds(pl.multiple_of(frame * frame_tokens, frame_tokens), frame_tokens)

    def cols_of(head):
        return pl.ds(pl.multiple_of(base + head * HEAD_DIM, HEAD_DIM), HEAD_DIM)

    scores = scores_of(q_ref[0, :, columns(0)], kbuf[rows, cols_of(0)])
    for head in range(heads):
        following = None
        if head + 1 < heads:
            following = scores_of(q_ref[0, :, columns(head + 1)], kbuf[rows, cols_of(head + 1)])
        new = row_max(scores)
        acc[head] = jnp.dot(
            weights_of(scores, new), widened(vbuf[rows, cols_of(head)]), preferred_element_type=jnp.float32
        )
        top[head] = new
        scores = following
    arrived(0, range(1, min(reach, frames - 1) + 1))
    for at_frame in range(1, frames - reach):
        arrived(at_frame, [at_frame + reach])
    listed_chunks(chosen, count, heads, base, q_ref, kbuf, vbuf, acc, top)
    lane = lax.broadcasted_iota(jnp.int32, (half, HEAD_DIM), 1)
    state = jnp.zeros((half, HEAD_DIM), jnp.float32)
    for head in range(heads):
        acc_out[0, :, columns(head)] = acc[head, :, :HEAD_DIM]
        state = jnp.where(lane == 2 * head, top[head], state)
        state = jnp.where(lane == 2 * head + 1, acc[head, :, HEAD_DIM:], state)
    state_out[0, 0] = state


def far_kernel(frames, heads, lengths, edge, tiles, counts, q_ref, acc_in, state_in, *refs):
    parts = 4 if edge else 2
    owns, others, rest = refs[:parts], refs[parts : 2 * parts], refs[2 * parts + edge :]
    out_ref, kbuf, vbuf, chosen, sems = rest
    seq = lax.axis_index("seq")
    step, group = pl.program_id(0), pl.program_id(1)
    frame = step * (frames - 1) if edge else step + 1
    half = q_ref.shape[1]
    behind = sum((distance - 1) * length for distance, length in zip(DISTANCES, lengths))
    beside = sum(lengths)

    def copies(core):
        first = 0
        for place, (own, other) in enumerate(zip(owns, others)):
            keys, values = (own, other) if core == 0 else (other, own)
            span = pl.ds(first, own.shape[0])
            first += own.shape[0]
            yield pltpu.make_async_copy(keys, kbuf.at[span, :], sems.at[2 * place])
            yield pltpu.make_async_copy(values, vbuf.at[span, :], sems.at[2 * place + 1])

    for core in (0, 1):

        @pl.when((step == 0) & (group == 0) & (seq == core))
        def _(core=core):
            for copy in copies(core):
                copy.start()

    count = jnp.int32(0)
    mine = lax.axis_index("frame") * frames + frame
    for direction in (0, 1):
        first_behind, first_beside = direction * behind, 2 * behind + direction * beside
        for rank, distance in enumerate(DISTANCES):
            place = frame if direction == 0 else frame - (frames - distance)
            next_to = frame == (0 if direction == 0 else frames - 1)
            crosses = (place >= 0) & (place < distance)
            live = counts[(mine * 2 + direction) * len(DISTANCES) + rank]
            for entry in range(lengths[rank]):
                keep = crosses & (entry < live)
                at = jnp.where(
                    next_to, first_beside + entry, first_behind + (place - (1 - direction)) * lengths[rank] + entry
                )
                chosen[count] = jnp.where(keep, at, 0)
                count = count + keep.astype(jnp.int32)
            first_behind += (distance - 1) * lengths[rank]
            first_beside += lengths[rank]
    for place in range(tiles):
        chosen[count + place] = 0

    for at_step, waited in ((0, slice(0, 6)), (1, slice(6, 8))):
        for core in (0, 1):

            @pl.when((step == at_step) & (group == 0) & (seq == core))
            def _(core=core, waited=waited):
                for copy in list(copies(core))[waited]:
                    copy.wait()

    spans = [pl.ds(pl.multiple_of(chosen[place] * TILE, TILE), TILE) for place in range(tiles)]
    biases = [jnp.where(place < count, jnp.float32(0.0), jnp.float32(-jnp.inf)) for place in range(tiles)]
    state = state_in[0, 0]

    def cols_of(head):
        return pl.ds(pl.multiple_of((group * heads + head) * HEAD_DIM, HEAD_DIM), HEAD_DIM)

    def scores_for(head):
        keys = jnp.concatenate([kbuf[span, cols_of(head)] for span in spans], axis=0)
        return scores_of(q_ref[0, :, columns(head)], keys)

    def from_state(lane):
        return jnp.broadcast_to(state[:, lane : lane + 1], (half, HEAD_DIM))

    scores = scores_for(0)
    for head in range(heads):
        following = scores_for(head + 1) if head + 1 < heads else None
        masked = jnp.concatenate(
            [scores[:, place * TILE : (place + 1) * TILE] + biases[place] for place in range(tiles)], axis=1
        )
        old = from_state(2 * head)
        new = jnp.maximum(old, row_max(masked))
        factor = jnp.exp2((old - new) * SCORE_SCALE)
        values = jnp.concatenate([vbuf[span, cols_of(head)] for span in spans], axis=0)
        mixed = jnp.dot(weights_of(masked, new), widened(values), preferred_element_type=jnp.float32)
        total = from_state(2 * head + 1) * factor + mixed[:, HEAD_DIM:]
        out_ref[0, :, columns(head)] = (
            (acc_in[0, :, columns(head)] * factor + mixed[:, :HEAD_DIM]) / total
        ).astype(jnp.bfloat16)
        scores = following


def per_device(queries, key_rows, value_rows, list_one, list_two, list_four, tile_counts):
    frames, half, width = queries.shape
    frame_total = list_one.shape[0]
    lengths = (list_one.shape[2], list_two.shape[2], list_four.shape[2])
    head_total = width // HEAD_DIM
    heads = max(h for h in (1, 2, 3) if head_total % h == 0)
    groups = head_total // heads
    parts = parts_of(lengths)
    slots = sum(len(part) for _, part in parts)
    lists = tuple(x.reshape(-1) for x in (list_one, list_two, list_four))
    counts = tile_counts.reshape(-1)
    listed = 2 * sum(lengths)
    devices = lax.axis_size("frame")
    swap = [(0, 1), (1, 0)]

    first = (lax.ppermute(key_rows, "seq", [(1, 0)]), lax.ppermute(value_rows, "seq", [(0, 1)]))
    second = (lax.ppermute(key_rows, "seq", [(0, 1)]), lax.ppermute(value_rows, "seq", [(1, 0)]))

    whole = pl.BlockSpec(memory_space=pltpu.VMEM)
    packed = pl.pallas_call(
        functools.partial(pack_kernel, frames, frame_total, lengths),
        out_shape=[jax.ShapeDtypeStruct((len(part), TILE, width), jnp.bfloat16) for _, part in parts],
        in_specs=[pl.BlockSpec(memory_space=pltpu.SMEM)] * 3 + [ANY] * 4,
        out_specs=[whole] * len(parts),
        scratch_shapes=[pltpu.SemaphoreType.DMA((slots,))],
        name="pack",
    )(*lists, key_rows, first[0], value_rows, first[1])

    routes = ([(i, i + 1) for i in range(devices - 1)], [(i + 1, i) for i in range(devices - 1)])
    sent = [
        lax.ppermute(x.reshape(-1, width), "frame", routes[direction]) for x, (direction, _) in zip(packed, parts)
    ]

    def cost(tokens):
        return pl.CostEstimate(
            flops=8 * frames * half * width * tokens,
            transcendentals=frames * half * head_total * tokens,
            bytes_accessed=40 * frames * half * width,
        )

    def block(f, g, *_):
        return (f, 0, g)

    q_spec = pl.BlockSpec((1, half, heads * HEAD_DIM), block)
    state_spec = pl.BlockSpec((1, 1, half, HEAD_DIM), lambda f, g, *_: (f, g, 0, 0))
    running = [
        pltpu.VMEM((heads, half, 2 * HEAD_DIM), jnp.float32),
        pltpu.VMEM((heads, half, HEAD_DIM), jnp.float32),
        pltpu.SMEM((listed + GROUP,), jnp.int32),
    ]
    params = pltpu.CompilerParams(vmem_limit_bytes=60 << 20)
    acc, state = pl.pallas_call(
        functools.partial(near_kernel, frames, heads, lengths),
        grid_spec=pltpu.PrefetchScalarGridSpec(
            num_scalar_prefetch=4,
            grid=(frames, groups),
            in_specs=[q_spec] + [ANY] * 6,
            out_specs=(q_spec, state_spec),
            scratch_shapes=[pltpu.VMEM((frames * 2 * half, width), jnp.bfloat16)] * 2
            + running
            + [pltpu.SemaphoreType.DMA((frames, 4))],
        ),
        out_shape=(
            jax.ShapeDtypeStruct(queries.shape, jnp.float32),
            jax.ShapeDtypeStruct((frames, groups, half, HEAD_DIM), jnp.float32),
        ),
        compiler_params=params,
        cost_estimate=cost(2 * half + listed * TILE // 2),
        name="near",
    )(*lists, counts, queries, key_rows, value_rows, *first, *second)

    behind = lax.optimization_barrier((acc, *sent[:2]))
    beside = lax.optimization_barrier((acc, *sent[2:]))
    acc = behind[0]
    own = [*behind[1:], *beside[1:]]
    other = [lax.ppermute(x, "seq", swap) for x in own]

    def far(edge, frame_of, steps, done):
        used = 4 if edge else 2
        rows = sum(x.shape[0] for x in own[:used])
        tiles = max(
            sum(length * ((f < d) + (f >= frames - d)) for d, length in zip(DISTANCES, lengths))
            for f in map(frame_of, range(steps))
        )
        far_block = lambda f, g, *_: (frame_of(f), 0, g)
        far_spec = pl.BlockSpec((1, half, heads * HEAD_DIM), far_block)
        far_state = pl.BlockSpec((1, 1, half, HEAD_DIM), lambda f, g, *_: (frame_of(f), g, 0, 0))
        return pl.pallas_call(
            functools.partial(far_kernel, frames, heads, lengths, edge, tiles),
            grid_spec=pltpu.PrefetchScalarGridSpec(
                num_scalar_prefetch=1,
                grid=(steps, groups),
                in_specs=[far_spec, far_spec, far_state] + [ANY] * (2 * used + len(done)),
                out_specs=far_spec,
                scratch_shapes=[pltpu.VMEM((rows, width), jnp.bfloat16)] * 2
                + [pltpu.SMEM((listed + tiles,), jnp.int32), pltpu.SemaphoreType.DMA((2 * used,))],
            ),
            out_shape=jax.ShapeDtypeStruct(queries.shape, jnp.bfloat16),
            input_output_aliases={4 + 2 * used: 0} if done else {},
            compiler_params=params,
            cost_estimate=cost(listed * TILE // 4),
            name="far_edge" if edge else "far_inner",
        )(counts, queries, acc, state, *own[:used], *other[:used], *done)

    inner = far(False, lambda f: f + 1, frames - 2, ())
    return far(True, lambda f: f * (frames - 1), 2, (inner,))


def solution(mesh):
    placed = P(("clips", "frame"), "seq", "head")
    listing = P("clips", None, None)
    return jax.shard_map(
        per_device,
        mesh=mesh,
        in_specs=(placed, placed, placed, listing, listing, listing, listing),
        out_specs=placed,
        check_vma=False,
    )
```
